32 devices in a mesh: dp: 8 (over z, core), seq: 4 (over y, x).
Axes of the slice: x: 2, y: 2, z: 4, core: 2. Of those that a mesh axis runs over, the one named last changes fastest.
Arguments:
- hidden_in: bfloat16 [8, 2048, 1088], P('dp', 'seq'), may hold values from -6 to 6
- segments: int32 [8, 2048], P('dp'), may hold values from 0 to 3, never falling along the last dimension, each value on 1 to 1024 neighbouring positions
- cotangent: bfloat16 [8, 2048, 1088], P('dp', 'seq'), may hold values from -6 to 6
- w_qkv: bfloat16 [27904, 128], P(('dp', 'seq')), may hold values from -0.1875 to 0.1875
- w_out: bfloat16 [9472, 128], P(('dp', 'seq')), may hold values from -1 to 1
- w_up: bfloat16 [37120, 128], P(('dp', 'seq')), may hold values from -0.1875 to 0.1875
- w_down: bfloat16 [37120, 128], P(('dp', 'seq')), may hold values from -0.09375 to 0.09375
- vectors: bfloat16 [256, 128], P(('dp', 'seq')), may hold values from -1.21 to 1.3
Outputs:
- hidden_out: bfloat16 [8, 2048, 1088], P('dp', 'seq')
- grad_in: float32 [8, 2048, 1088], P('dp', 'seq')
- grad_qkv: float32 [27904, 128], P(('dp', 'seq'))
- grad_out_proj: float32 [9472, 128], P(('dp', 'seq'))
- grad_up: float32 [37120, 128], P(('dp', 'seq'))
- grad_down: float32 [37120, 128], P(('dp', 'seq'))
- grad_vectors: float32 [256, 128], P(('dp', 'seq'))
The draws below stay inside these ranges and needn't reach their ends.
Inputs may be any that keep to these rules, and one draw needn't show every extreme that they name: `segments`: in each sequence the segment numbers never fall; a segment covers 1 to 1024 positions and one covers exactly that many.
All inputs are finite; a program needn't handle non-finite values.
Results may differ from the reference program's by a relative error of at most 0.019.
Values may be sent and summed in bfloat16 or wider, within the bound.
A program may use at most 256 MiB of HBM per device.

```python
import math
import jax
import jax.numpy as jnp
import numpy as np
from jax import lax

D = 1088
HEADS = 17
FF = 4352
LENGTH = 2048
SEQS = 8
QKV_ROWS = 27904
OUT_ROWS = 9472
MLP_ROWS = 37120
VEC_ROWS = 256


def draw_vectors(key, part):
    total_len = VEC_ROWS * 128
    position = jnp.arange(total_len, dtype=jnp.int32)
    is_gain = (position < D) | (position >= 5 * D) & (position < 6 * D)
    base_draw = jnp.clip(jax.random.normal(key, (total_len,), jnp.float32), -3.0, 3.0)
    values = jnp.where(is_gain, 1.0 + 0.1 * base_draw, 0.4 * base_draw)
    return values.reshape(VEC_ROWS, 128).astype(jnp.bfloat16)


def levels(key, shape, pieces, low, largest):
    gain, own = 1.0, jax.random.fold_in(key, 6)
    for axis_at, parts in pieces:
        steps = jnp.exp(jax.random.uniform(jax.random.fold_in(own, axis_at), (parts,), jnp.float32, low / len(pieces), largest / len(pieces)))
        gain = gain * jnp.repeat(steps, shape[axis_at] // parts).reshape([-1 if axis == axis_at else 1 for axis in range(len(shape))])
    return gain


def profile(count, total, limit, lean):
    weights = [(1 << 20) // math.isqrt(rank ** lean) + 1 for rank in range(2, count + 1)]
    rest, counts = total - limit - (count - 1), [1] * (count - 1)
    while rest > 0:
        candidates = [i for i in range(count - 1) if counts[i] < limit]
        mass, budget = sum([weights[i] for i in candidates]), rest
        for i in candidates:
            addition = min(limit - counts[i], max(1, budget * weights[i] // mass), rest)
            counts[i] = counts[i] + addition
            rest = rest - addition
    return np.array([limit] + counts)


def ragged_sizes(stream_key, amount, total, most, lean):
    if amount == 2:
        one = jax.random.randint(stream_key, (), max(1, total - most), min(most, total - 1) + 1)
        return jnp.stack([one, total - one])
    sizes = jnp.asarray(profile(amount, total, most, lean), jnp.int32)
    couples = (amount - 1) // 2
    giver, sink = sizes[1:1 + 2 * couples:2], sizes[2:2 + 2 * couples:2]
    room = jnp.minimum(giver - 1, most - sink)
    passed = jax.random.randint(jax.random.fold_in(stream_key, 1), (couples,), 0, 1 << 20) % (room + 1)
    sizes = sizes.at[1:1 + 2 * couples:2].set(giver - passed).at[2:2 + 2 * couples:2].set(sink + passed)
    return sizes[jax.random.permutation(jax.random.fold_in(stream_key, 2), amount)]


def bell_draw(own_key, extent, scale, limit, split=(), kind=jnp.bfloat16):
    entries = jax.random.normal(own_key, extent, jnp.float32) * scale
    if len(split) > 0:
        entries = levels(own_key, extent, split, -0.22, 0.18) * entries
    return jnp.clip(entries, min=-limit, max=limit).astype(kind)


def setup_inputs(seed: int = 0) -> dict:
    key_list = jax.random.split(jax.random.key(seed), 9)
    hidden_in = bell_draw(key_list[0], (SEQS, LENGTH, D), 1.0, 6.0, ((0, 8), (1, 4)))
    segments = jax.vmap(lambda own: jnp.searchsorted(jnp.cumsum(ragged_sizes(own, 4, LENGTH, LENGTH // 2, 0)), jnp.arange(LENGTH), side="right"))(jax.random.split(key_list[1], SEQS)).reshape((SEQS, LENGTH)).astype(jnp.int32)
    cotangent = bell_draw(key_list[2], (SEQS, LENGTH, D), 1.0, 6.0, ((0, 8), (1, 4)))
    w_qkv = bell_draw(key_list[3], (QKV_ROWS, 128), D ** -0.5, 0.1875, ((0, 32),))
    w_out = bell_draw(key_list[4], (OUT_ROWS, 128), (D // 32) ** -0.5, 1.0, ((0, 32),))
    w_up = bell_draw(key_list[5], (MLP_ROWS, 128), D ** -0.5, 0.1875, ((0, 32),))
    w_down = bell_draw(key_list[6], (MLP_ROWS, 128), FF ** -0.5, 0.09375, ((0, 32),))
    vectors = draw_vectors(jax.random.fold_in(key_list[8], 71), 0)
    return {"hidden_in": hidden_in, "segments": segments, "cotangent": cotangent, "w_qkv": w_qkv, "w_out": w_out, "w_up": w_up, "w_down": w_down, "vectors": vectors}


@jax.custom_vjp
def low(v):
    return lax.optimization_barrier(v.astype(jnp.bfloat16)).astype(jnp.float32)

@jax.custom_vjp
def low_back(v):
    return v

def low_keep(v):
    return (low(v), None)

def low_pass(kept, grad):
    return (grad,)

def back_keep(v):
    return (v, None)

def back_low(kept, grad):
    return (low(grad),)
low.defvjp(low_keep, low_pass)
low_back.defvjp(back_keep, back_low)

def matmul(left, right):
    return jnp.dot(left, right, precision=lax.Precision.HIGHEST)

def layer_norm(values, gain_vec, shift_vec):
    centre = lax.optimization_barrier(jnp.mean(values, axis=-1, keepdims=True))
    centred = values - centre
    spread = lax.optimization_barrier(jnp.mean(centred * centred, axis=-1, keepdims=True))
    return centred * lax.rsqrt(spread + 1e-05) * gain_vec + shift_vec

def unpack(flat_values, model_width, hidden_units):
    gain_one = flat_values[0:model_width]
    shift_one = flat_values[model_width:2 * model_width]
    bias_query = flat_values[2 * model_width:3 * model_width]
    bias_value = flat_values[3 * model_width:4 * model_width]
    bias_proj = flat_values[4 * model_width:5 * model_width]
    gain_two = flat_values[5 * model_width:6 * model_width]
    shift_two = flat_values[6 * model_width:7 * model_width]
    bias_up = flat_values[7 * model_width:7 * model_width + hidden_units]
    bias_down = flat_values[7 * model_width + hidden_units:8 * model_width + hidden_units]
    return (gain_one, shift_one, bias_query, bias_value, bias_proj, gain_two, shift_two, bias_up, bias_down)

def take_matrix(flat_rows, row_count, col_count):
    return flat_rows.reshape(-1)[:row_count * col_count].reshape(row_count, col_count)

def layer_forward(tokens, seg_ids, w_qkv, w_out, w_up, w_down, flat_vec):
    model_width = tokens.shape[1]
    length = tokens.shape[0]
    head_dim = model_width // HEADS
    score_scale = head_dim ** (-0.5)
    gain_one, shift_one, bias_query, bias_value, bias_proj, gain_two, shift_two, bias_up, bias_down = unpack(flat_vec.reshape(-1), model_width, w_up.shape[1])
    normed = low(layer_norm(tokens, gain_one, shift_one))
    packed = matmul(normed, w_qkv)
    queries = low(low_back(packed[:, :model_width] + bias_query)).reshape(length, HEADS, head_dim)
    key_rows = low(low_back(packed[:, model_width:2 * model_width])).reshape(length, HEADS, head_dim)
    value_rows = low(low_back(packed[:, 2 * model_width:] + bias_value)).reshape(length, HEADS, head_dim)
    scores = low_back(score_scale * jnp.einsum('qhd,khd->hqk', queries, key_rows, precision=lax.Precision.HIGHEST))
    places = jnp.arange(length, dtype=jnp.int32)
    visible = (places[:, None] >= places[None, :]) & (seg_ids[:, None] == seg_ids[None, :])
    scores = jnp.where(visible[None], scores, -1e+30)
    weights = low(jax.nn.softmax(scores, axis=-1))
    mixed = jnp.einsum('hqk,khd->qhd', weights, value_rows, precision=lax.Precision.HIGHEST).reshape(length, model_width)
    attended = low(low_back(mixed))
    middle = tokens + low_back(matmul(attended, w_out)) + bias_proj
    normed_two = low(layer_norm(middle, gain_two, shift_two))
    before = low_back(matmul(normed_two, w_up) + bias_up)
    active = low(jax.nn.gelu(before))
    return middle + matmul(active, w_down) + bias_down

def reference(hidden_in, segments, cotangent, w_qkv, w_out, w_up, w_down, vectors):
    qkv_f = w_qkv.astype(jnp.float32)
    out_f = w_out.astype(jnp.float32)
    up_f = w_up.astype(jnp.float32)
    down_f = w_down.astype(jnp.float32)
    vec_f = vectors.astype(jnp.float32)

    def per_sequence(summed, items):
        tokens, seg_ids, cot_rows = items

        def forward_of(rows_in, p_qkv, p_out, p_up, p_down, p_vec):
            model_width = rows_in.shape[1]
            return layer_forward(rows_in, seg_ids, take_matrix(p_qkv, model_width, 3 * model_width), take_matrix(p_out, model_width, model_width), take_matrix(p_up, model_width, FF), take_matrix(p_down, FF, model_width), p_vec)
        result, pull = jax.vjp(forward_of, tokens.astype(jnp.float32), qkv_f, out_f, up_f, down_f, vec_f)
        grads = pull(cot_rows.astype(jnp.float32))
        summed = (summed[0] + grads[1], summed[1] + grads[2], summed[2] + grads[3], summed[3] + grads[4], summed[4] + grads[5])
        return (summed, (result.astype(jnp.bfloat16), grads[0]))
    initial = (jnp.zeros(qkv_f.shape, jnp.float32), jnp.zeros(out_f.shape, jnp.float32), jnp.zeros(up_f.shape, jnp.float32), jnp.zeros(down_f.shape, jnp.float32), jnp.zeros(vec_f.shape, jnp.float32))
    summed, (outputs, input_grads) = lax.scan(per_sequence, initial, (hidden_in, segments, cotangent))
    return (outputs, input_grads, summed[0], summed[1], summed[2], summed[3], summed[4])
```

```python
import jax
import jax.numpy as jnp
from jax import lax
from jax.experimental import pallas as pl
from jax.experimental.pallas import tpu as pltpu
from jax.sharding import PartitionSpec as P

HEADS = 17
FF = 4352


eps_norm = 1e-05
masked_score = -1e30


def layer_norm(values, gain_vec, shift_vec):
    centre = jnp.mean(values, axis=-1, keepdims=True)
    centred = values - centre
    spread = jnp.mean(centred * centred, axis=-1, keepdims=True)
    return centred * lax.rsqrt(spread + eps_norm) * gain_vec + shift_vec


def unpack(flat_values, model_width, hidden_units):
    gain_one = flat_values[0:model_width]
    shift_one = flat_values[model_width : 2 * model_width]
    bias_query = flat_values[2 * model_width : 3 * model_width]
    bias_value = flat_values[3 * model_width : 4 * model_width]
    bias_proj = flat_values[4 * model_width : 5 * model_width]
    gain_two = flat_values[5 * model_width : 6 * model_width]
    shift_two = flat_values[6 * model_width : 7 * model_width]
    bias_up = flat_values[7 * model_width : 7 * model_width + hidden_units]
    bias_down = flat_values[7 * model_width + hidden_units : 8 * model_width + hidden_units]
    return (
        gain_one,
        shift_one,
        bias_query,
        bias_value,
        bias_proj,
        gain_two,
        shift_two,
        bias_up,
        bias_down,
    )


def take_matrix(flat_rows, row_count, col_count):
    return flat_rows.reshape(-1)[: row_count * col_count].reshape(row_count, col_count)


def to_flat(grad_matrix, row_count):
    flat_values = grad_matrix.reshape(-1)
    return jnp.pad(flat_values, (0, row_count * 128 - flat_values.shape[0])).reshape(row_count, 128)


def shape_weights(gathered, model_width):
    return (
        take_matrix(gathered[0], model_width, 3 * model_width),
        take_matrix(gathered[1], model_width, model_width),
        take_matrix(gathered[2], model_width, FF),
        take_matrix(gathered[3], FF, model_width),
        gathered[4],
    )


def fetch(*flat_weights):
    return tuple(lax.all_gather(flat, ("dp", "seq"), axis=0, tiled=True) for flat in flat_weights)


def reduce_mlp(grad_up_flat, grad_down_flat):
    by_row = (
        lax.psum_scatter(
            grad_up_flat.astype(jnp.bfloat16), "dp", scatter_dimension=0, tiled=True
        ).astype(jnp.float32),
        lax.psum_scatter(
            grad_down_flat.astype(jnp.bfloat16), "dp", scatter_dimension=0, tiled=True
        ).astype(jnp.float32),
    )
    return (
        lax.psum_scatter(
            by_row[0].astype(jnp.bfloat16), "seq", scatter_dimension=0, tiled=True
        ).astype(jnp.float32),
        lax.psum_scatter(
            by_row[1].astype(jnp.bfloat16), "seq", scatter_dimension=0, tiled=True
        ).astype(jnp.float32),
    )


def reduce_attention(grad_qkv_flat, grad_out_flat, grad_vec_flat):
    by_row = (
        lax.psum_scatter(
            grad_qkv_flat.astype(jnp.bfloat16), "dp", scatter_dimension=0, tiled=True
        ).astype(jnp.float32),
        lax.psum_scatter(
            grad_out_flat.astype(jnp.bfloat16), "dp", scatter_dimension=0, tiled=True
        ).astype(jnp.float32),
        lax.psum_scatter(
            grad_vec_flat.astype(jnp.bfloat16), "dp", scatter_dimension=0, tiled=True
        ).astype(jnp.float32),
    )
    return (
        lax.psum_scatter(
            by_row[0].astype(jnp.bfloat16), "seq", scatter_dimension=0, tiled=True
        ).astype(jnp.float32),
        lax.psum_scatter(
            by_row[1].astype(jnp.bfloat16), "seq", scatter_dimension=0, tiled=True
        ).astype(jnp.float32),
        lax.psum_scatter(
            by_row[2].astype(jnp.bfloat16), "seq", scatter_dimension=0, tiled=True
        ).astype(jnp.float32),
    )


KEY_TILE = 256
LANES = 128


def contract(left, right, left_dim, right_dim):
    return lax.dot_general(
        left, right, (((left_dim,), (right_dim,)), ((), ())), preferred_element_type=jnp.float32
    )


def stack_pair(block):
    half = block.shape[1] // 2
    lane = lax.broadcasted_iota(jnp.int32, block.shape, 1)
    zero = jnp.zeros_like(block)
    return jnp.concatenate(
        [jnp.where(lane < half, block, zero), jnp.where(lane < half, zero, block)], axis=0
    )


def unstack_pair(wide, rows):
    half = wide.shape[0] // 2
    return jnp.concatenate([wide[:half, :rows], wide[half:, rows:]], axis=0)


def masked_scores(bounds_ref, keys, stacked, starts, places, offset):
    scores = contract(keys, stacked, 1, 1)
    key_places = offset + lax.broadcasted_iota(jnp.int32, scores.shape, 0)
    visible = (key_places >= starts) & (key_places <= places)
    return jnp.where(visible, scores, masked_score)


def forward_kernel(
    bounds_ref, q_ref, k_ref, v_ref, starts_ref, places_ref, o_ref, lse_ref, top, total, acc
):
    rows = q_ref.shape[0]
    stacked = stack_pair(q_ref[...])
    starts = starts_ref[...]
    places = places_ref[...]
    top[...] = jnp.full_like(top, masked_score)
    total[...] = jnp.zeros_like(total)
    acc[...] = jnp.zeros_like(acc)

    def step(tile, carry):
        offset = pl.multiple_of(tile * KEY_TILE, KEY_TILE)
        keys = k_ref[pl.ds(offset, KEY_TILE), :]
        values = v_ref[pl.ds(offset, KEY_TILE), :]
        scores = masked_scores(bounds_ref, keys, stacked, starts, places, offset)
        old_top = top[...]
        new_top = jnp.maximum(old_top, jnp.max(scores, axis=0, keepdims=True))
        weights = jnp.exp(scores - new_top)
        factor = jnp.exp(old_top - new_top)
        top[...] = new_top
        total[...] = total[...] * factor + jnp.sum(weights, axis=0, keepdims=True)
        acc[...] = acc[...] * factor + contract(values, weights.astype(jnp.bfloat16), 0, 0)
        return carry

    lax.fori_loop(bounds_ref[0], bounds_ref[1], step, 0)
    lse_ref[0] = top[...] + jnp.log(total[...])
    o_ref[...] = unstack_pair(acc[...] / total[...], rows).T


def backward_kernel(
    bounds_ref, q_ref, k_ref, v_ref, g_ref, o_ref, lse_ref, starts_ref, places_ref,
    dq_ref, dk_ref, dv_ref, acc,
):
    rows = q_ref.shape[0]
    stacked = stack_pair(q_ref[...])
    grads = g_ref[...]
    stacked_g = stack_pair(grads)
    mixed = (grads.astype(jnp.float32) * o_ref[...]).T
    half = mixed.shape[0] // 2
    row_dots = jnp.concatenate(
        [
            jnp.sum(mixed[:half], axis=0, keepdims=True),
            jnp.sum(mixed[half:], axis=0, keepdims=True),
        ],
        axis=1,
    )
    starts = starts_ref[...]
    places = places_ref[...]
    totals = lse_ref[0]
    acc[...] = jnp.zeros_like(acc)
    dk_ref[...] = jnp.zeros_like(dk_ref)
    dv_ref[...] = jnp.zeros_like(dv_ref)

    def step(tile, carry):
        offset = pl.multiple_of(tile * KEY_TILE, KEY_TILE)
        keys = k_ref[pl.ds(offset, KEY_TILE), :]
        values = v_ref[pl.ds(offset, KEY_TILE), :]
        scores = masked_scores(bounds_ref, keys, stacked, starts, places, offset)
        probs = jnp.exp(scores - totals)
        d_probs = contract(values, stacked_g, 1, 1)
        d_scores = (probs * (d_probs - row_dots)).astype(jnp.bfloat16)
        dv_ref[pl.ds(offset, KEY_TILE), :] = contract(
            probs.astype(jnp.bfloat16), stacked_g, 1, 0
        ).astype(dv_ref.dtype)
        dk_ref[pl.ds(offset, KEY_TILE), :] = contract(d_scores, stacked, 1, 0).astype(dk_ref.dtype)
        acc[...] += contract(keys, d_scores, 0, 0)
        return carry

    lax.fori_loop(bounds_ref[0], bounds_ref[1], step, 0)
    dq_ref[...] = unstack_pair(acc[...], rows).T


def column_spec(rows):
    return pl.BlockSpec((rows, LANES), lambda pair, bounds: (0, pair))


def whole_spec(cols):
    return pl.BlockSpec((1, cols), lambda pair, bounds: (0, 0))


def pair_spec(cols):
    return pl.BlockSpec((1, 1, cols), lambda pair, bounds: (pair, 0, 0))


def attend(bounds, queries, keys, values, starts, places):
    rows, width = queries.shape
    length = keys.shape[0]
    pairs = width // LANES
    return pl.pallas_call(
        forward_kernel,
        grid_spec=pltpu.PrefetchScalarGridSpec(
            num_scalar_prefetch=1,
            grid=(pairs,),
            in_specs=[
                column_spec(rows), column_spec(length), column_spec(length),
                whole_spec(2 * rows), whole_spec(2 * rows),
            ],
            out_specs=[column_spec(rows), pair_spec(2 * rows)],
            scratch_shapes=[
                pltpu.VMEM((1, 2 * rows), jnp.float32),
                pltpu.VMEM((1, 2 * rows), jnp.float32),
                pltpu.VMEM((LANES, 2 * rows), jnp.float32),
            ],
        ),
        out_shape=[
            jax.ShapeDtypeStruct((rows, width), jnp.float32),
            jax.ShapeDtypeStruct((pairs, 1, 2 * rows), jnp.float32),
        ],
        compiler_params=pltpu.CompilerParams(vmem_limit_bytes=40 * 1024 * 1024),
        cost_estimate=pl.CostEstimate(
            flops=8 * rows * length * width, bytes_accessed=8 * length * width,
            transcendentals=rows * length * width // 64,
        ),
        name="attention_forward",
    )(bounds, queries, keys, values, starts, places)


def attend_back(bounds, queries, keys, values, grads, mixed, totals, starts, places):
    rows, width = queries.shape
    length = keys.shape[0]
    pairs = width // LANES
    return pl.pallas_call(
        backward_kernel,
        grid_spec=pltpu.PrefetchScalarGridSpec(
            num_scalar_prefetch=1,
            grid=(pairs,),
            in_specs=[
                column_spec(rows), column_spec(length), column_spec(length),
                column_spec(rows), column_spec(rows), pair_spec(2 * rows),
                whole_spec(2 * rows), whole_spec(2 * rows),
            ],
            out_specs=[column_spec(rows), column_spec(length), column_spec(length)],
            scratch_shapes=[pltpu.VMEM((LANES, 2 * rows), jnp.float32)],
        ),
        out_shape=[
            jax.ShapeDtypeStruct((rows, width), jnp.float32),
            jax.ShapeDtypeStruct((length, width), jnp.bfloat16),
            jax.ShapeDtypeStruct((length, width), jnp.bfloat16),
        ],
        compiler_params=pltpu.CompilerParams(vmem_limit_bytes=48 * 1024 * 1024),
        cost_estimate=pl.CostEstimate(
            flops=20 * rows * length * width, bytes_accessed=12 * length * width,
            transcendentals=rows * length * width // 64,
        ),
        name="attention_backward",
    )(bounds, queries, keys, values, grads, mixed, totals, starts, places)


def body(hidden_in, segments, cotangent, w_qkv, w_out, w_up, w_down, vectors):
    tok_rows = hidden_in.shape[1]
    model_width = hidden_in.shape[2]
    head_dim = model_width // HEADS
    score_scale = head_dim ** (-0.5)
    length = segments.shape[1]
    spread_count = lax.axis_size("dp") * lax.axis_size("seq")
    seg_row = segments[0]
    query_first = lax.axis_index("seq") * tok_rows
    query_places = query_first + jnp.arange(tok_rows, dtype=jnp.int32)
    query_segs = lax.dynamic_slice_in_dim(seg_row, query_first, tok_rows)
    fwd_gathered = fetch(w_qkv, w_out, w_up, w_down, vectors)
    fwd_weights = shape_weights(fwd_gathered, model_width)
    hidden_units = FF
    (
        gain_one,
        shift_one,
        bias_query,
        bias_value,
        bias_proj,
        gain_two,
        shift_two,
        bias_up,
        bias_down,
    ) = unpack(fwd_weights[4].reshape(-1).astype(jnp.float32), model_width, hidden_units)
    tokens = hidden_in[0].astype(jnp.float32)
    normed_f, pull_one = jax.vjp(layer_norm, tokens, gain_one, shift_one)
    normed = normed_f.astype(jnp.bfloat16)
    packed = jnp.dot(normed, fwd_weights[0], preferred_element_type=jnp.float32)
    queries = (packed[:, :model_width] + bias_query).astype(jnp.bfloat16)
    key_rows = packed[:, model_width : 2 * model_width].astype(jnp.bfloat16)
    value_rows = (packed[:, 2 * model_width :] + bias_value).astype(jnp.bfloat16)
    pair_width = pl.cdiv(model_width, LANES) * LANES

    def widen(matrix):
        return jnp.pad(matrix, ((0, 0), (0, pair_width - matrix.shape[1])))

    queries = widen(queries * jnp.bfloat16(score_scale))
    key_rows = widen(key_rows)
    value_rows = widen(value_rows)
    query_starts = jnp.sum(
        (seg_row[None, :] < query_segs[:, None]).astype(jnp.int32), axis=1, dtype=jnp.int32
    )
    bounds = jnp.stack([query_starts[0] // KEY_TILE, pl.cdiv(query_first + tok_rows, KEY_TILE)])
    starts = jnp.tile(query_starts, 2)[None]
    places = jnp.tile(query_places, 2)[None]
    key_all = lax.all_gather(key_rows, "seq", axis=0, tiled=True)
    value_all = lax.all_gather(value_rows, "seq", axis=0, tiled=True)
    attended_f, log_total = attend(bounds, queries, key_all, value_all, starts, places)
    attended = attended_f[:, :model_width].astype(jnp.bfloat16)
    middle = (
        tokens + jnp.dot(attended, fwd_weights[1], preferred_element_type=jnp.float32) + bias_proj
    )
    normed_two_f, pull_two = jax.vjp(layer_norm, middle, gain_two, shift_two)
    normed_two = normed_two_f.astype(jnp.bfloat16)
    before = jnp.dot(normed_two, fwd_weights[2], preferred_element_type=jnp.float32) + bias_up
    active_f, pull_gelu = jax.vjp(jax.nn.gelu, before)
    active = active_f.astype(jnp.bfloat16)
    result = (
        middle + jnp.dot(active, fwd_weights[3], preferred_element_type=jnp.float32) + bias_down
    )
    hidden_out = result.astype(jnp.bfloat16)[None]
    back_weights = fwd_weights
    cot_rows = cotangent[0]
    cot_float = cot_rows.astype(jnp.float32)
    grad_down_full = jnp.dot(active.T, cot_rows, preferred_element_type=jnp.float32)
    d_bias_down = jnp.sum(cot_float, axis=0)
    d_active = jnp.dot(cot_rows, back_weights[3].T, preferred_element_type=jnp.float32)
    d_before = pull_gelu(d_active)[0].astype(jnp.bfloat16)
    d_bias_up = jnp.sum(d_before.astype(jnp.float32), axis=0)
    grad_up_full = jnp.dot(normed_two.T, d_before, preferred_element_type=jnp.float32)
    d_normed_two = jnp.dot(d_before, back_weights[2].T, preferred_element_type=jnp.float32)
    d_middle_norm, d_gain_two, d_shift_two = pull_two(d_normed_two)
    d_middle = cot_float + d_middle_norm
    mlp_grads = reduce_mlp(
        to_flat(grad_up_full, w_up.shape[0] * spread_count),
        to_flat(grad_down_full, w_down.shape[0] * spread_count),
    )
    d_proj = d_middle.astype(jnp.bfloat16)
    d_bias_proj = jnp.sum(d_middle, axis=0)
    grad_out_full = jnp.dot(attended.T, d_proj, preferred_element_type=jnp.float32)
    d_attended = jnp.dot(d_proj, back_weights[1].T, preferred_element_type=jnp.float32).astype(
        jnp.bfloat16
    )
    dq_sum, key_terms, value_terms = attend_back(
        bounds, queries, key_all, value_all, widen(d_attended), attended_f, log_total, starts,
        places,
    )
    d_key = lax.psum_scatter(key_terms, "seq", scatter_dimension=0, tiled=True)[:, :model_width]
    d_value = lax.psum_scatter(value_terms, "seq", scatter_dimension=0, tiled=True)[:, :model_width]
    d_query = (score_scale * dq_sum[:, :model_width]).astype(jnp.bfloat16)
    d_packed = jnp.concatenate([d_query, d_key, d_value], axis=1)
    grad_qkv_full = jnp.dot(normed.T, d_packed, preferred_element_type=jnp.float32)
    d_normed = jnp.dot(d_packed, back_weights[0].T, preferred_element_type=jnp.float32)
    d_tokens_norm, d_gain_one, d_shift_one = pull_one(d_normed)
    grad_in = (d_middle + d_tokens_norm)[None]
    vector_grads = jnp.concatenate(
        [
            d_gain_one,
            d_shift_one,
            jnp.sum(d_query.astype(jnp.float32), axis=0),
            jnp.sum(d_value.astype(jnp.float32), axis=0),
            d_bias_proj,
            d_gain_two,
            d_shift_two,
            d_bias_up,
            d_bias_down,
        ]
    )
    attn_grads = reduce_attention(
        to_flat(grad_qkv_full, w_qkv.shape[0] * spread_count),
        to_flat(grad_out_full, w_out.shape[0] * spread_count),
        to_flat(vector_grads, vectors.shape[0] * spread_count),
    )
    return (
        hidden_out,
        grad_in,
        attn_grads[0],
        attn_grads[1],
        mlp_grads[0],
        mlp_grads[1],
        attn_grads[2],
    )


def solution(mesh):
    return jax.shard_map(
        body,
        mesh=mesh,
        in_specs=(
            P("dp", "seq", None),
            P("dp", None),
            P("dp", "seq", None),
            P(("dp", "seq"), None),
            P(("dp", "seq"), None),
            P(("dp", "seq"), None),
            P(("dp", "seq"), None),
            P(("dp", "seq"), None),
        ),
        out_specs=(
            P("dp", "seq", None),
            P("dp", "seq", None),
            P(("dp", "seq"), None),
            P(("dp", "seq"), None),
            P(("dp", "seq"), None),
            P(("dp", "seq"), None),
            P(("dp", "seq"), None),
        ),
        check_vma=False,
    )
```

```python
import functools
import math

import jax
import jax.numpy as jnp
from jax import lax
from jax.experimental import pallas as pl
from jax.experimental.pallas import tpu as pltpu
from jax.sharding import PartitionSpec as P

HEADS = 17
FF = 4352


eps_norm = 1e-05
masked_score = -1e30


def layer_norm(values, gain_vec, shift_vec):
    centre = jnp.mean(values, axis=-1, keepdims=True)
    centred = values - centre
    spread = jnp.mean(centred * centred, axis=-1, keepdims=True)
    return centred * lax.rsqrt(spread + eps_norm) * gain_vec + shift_vec


def unpack(flat_values, model_width, hidden_units):
    gain_one = flat_values[0:model_width]
    shift_one = flat_values[model_width : 2 * model_width]
    bias_query = flat_values[2 * model_width : 3 * model_width]
    bias_value = flat_values[3 * model_width : 4 * model_width]
    bias_proj = flat_values[4 * model_width : 5 * model_width]
    gain_two = flat_values[5 * model_width : 6 * model_width]
    shift_two = flat_values[6 * model_width : 7 * model_width]
    bias_up = flat_values[7 * model_width : 7 * model_width + hidden_units]
    bias_down = flat_values[7 * model_width + hidden_units : 8 * model_width + hidden_units]
    return (
        gain_one,
        shift_one,
        bias_query,
        bias_value,
        bias_proj,
        gain_two,
        shift_two,
        bias_up,
        bias_down,
    )


def take_matrix(flat_rows, row_count, col_count):
    return flat_rows.reshape(-1)[: row_count * col_count].reshape(row_count, col_count)


def to_flat(grad_matrix, row_count):
    flat_values = grad_matrix.reshape(-1)
    return jnp.pad(flat_values, (0, row_count * 128 - flat_values.shape[0])).reshape(row_count, 128)


def shape_weights(gathered, model_width):
    return (
        take_matrix(gathered[0], model_width, 3 * model_width),
        take_matrix(gathered[1], model_width, model_width),
        take_matrix(gathered[2], model_width, FF),
        take_matrix(gathered[3], FF, model_width),
        gathered[4],
    )


def cyclic(size, stride, count, shift):
    pairs = []
    for source in range(count):
        place = (source // stride) % size
        pairs.append((source, source + (((place + shift) % size) - place) * stride))
    return pairs


def steps_of():
    depth = lax.axis_size("dp") // 2
    side = math.isqrt(lax.axis_size("seq"))
    return {
        "z": ("dp", depth, 2),
        "core": ("dp", 2, 1),
        "outer": ("seq", side, side),
        "inner": ("seq", side, 1),
    }


def position(step):
    name, size, stride = step
    return (lax.axis_index(name) // stride) % size


def shifted(values, step, shift):
    name, size, stride = step
    return lax.ppermute(values, name, cyclic(size, stride, lax.axis_size(name), shift))


def sum_over(values, step, dim):
    size = step[1]
    mine = position(step)
    total = lax.dynamic_index_in_dim(values, mine, dim, keepdims=False).astype(jnp.float32)
    for shift in range(1, size):
        piece = lax.dynamic_index_in_dim(values, (mine + shift) % size, dim, keepdims=False)
        total = total + shifted(piece, step, shift).astype(jnp.float32)
    return total


def collect(values, step, dim):
    size = step[1]
    mine = position(step)
    pieces = [values] + [shifted(values, step, shift) for shift in range(1, size)]
    return jnp.stack([lax.select_n((mine - at) % size, *pieces) if size > 2 else
                      jnp.where(mine == at, pieces[0], pieces[1]) for at in range(size)], axis=dim)


def scatter_sum(flat, kind=jnp.bfloat16):
    steps = steps_of()
    depth, side = steps["z"][1], steps["outer"][1]
    rows = flat.shape[0] // (2 * depth * side * side)
    parts = flat.astype(kind).reshape(depth, 2, side, side, rows, flat.shape[1])
    parts = sum_over(parts, steps["core"], 1).astype(kind)
    one = sum_over(parts[: depth // 2], steps["inner"], 2).astype(kind)
    two = sum_over(parts[depth // 2 :], steps["outer"], 1).astype(kind)
    one = sum_over(one, steps["outer"], 1).astype(kind)
    two = sum_over(two, steps["inner"], 1).astype(kind)
    return sum_over(jnp.concatenate([one, two], axis=0), steps["z"], 0)


def gather_all(flat):
    steps = steps_of()
    depth, side = steps["z"][1], steps["outer"][1]
    lines = collect(flat, steps["z"], 0)
    one = collect(lines[: depth // 2], steps["outer"], 1)
    two = collect(lines[depth // 2 :], steps["inner"], 1)
    one = collect(one, steps["inner"], 2)
    two = collect(two, steps["outer"], 1)
    parts = jnp.concatenate([one, two], axis=0)
    return collect(parts, steps["core"], 1).reshape(-1, flat.shape[1])


def fetch(*flat_weights):
    return tuple(gather_all(flat) for flat in flat_weights)


SEGMENT_MOST = 1024
LANES = 128


def contract(left, right, left_dim, right_dim):
    return lax.dot_general(
        left, right, (((left_dim,), (right_dim,)), ((), ())), preferred_element_type=jnp.float32
    )


def stack_pair(block):
    half = block.shape[1] // 2
    lane = lax.broadcasted_iota(jnp.int32, block.shape, 1)
    zero = jnp.zeros_like(block)
    return jnp.concatenate(
        [jnp.where(lane < half, block, zero), jnp.where(lane < half, zero, block)], axis=0
    )


def unstack_pair(wide, rows):
    half = wide.shape[0] // 2
    return jnp.concatenate([wide[:half, :rows], wide[half:, rows:]], axis=0)


def masked_scores(bounds_ref, keys, stacked, starts, places, offset):
    scores = contract(keys, stacked, 1, 1)
    key_places = offset + lax.broadcasted_iota(jnp.int32, scores.shape, 0)
    visible = (key_places >= starts) & (key_places <= places)
    return jnp.where(visible, scores, masked_score)


def forward_kernel(
    tile_rows, bounds_ref, q_ref, k_ref, v_ref, starts_ref, places_ref, o_ref, lse_ref, top, total, acc
):
    rows = q_ref.shape[0]
    stacked = stack_pair(q_ref[...])
    starts = starts_ref[...]
    places = places_ref[...]
    top[...] = jnp.full_like(top, masked_score)
    total[...] = jnp.zeros_like(total)
    acc[...] = jnp.zeros_like(acc)

    def step(tile, carry):
        offset = pl.multiple_of(tile * tile_rows, tile_rows)
        keys = k_ref[pl.ds(offset, tile_rows), :]
        values = v_ref[pl.ds(offset, tile_rows), :]
        scores = masked_scores(bounds_ref, keys, stacked, starts, places, offset)
        old_top = top[...]
        new_top = jnp.maximum(old_top, jnp.max(scores, axis=0, keepdims=True))
        weights = jnp.exp(scores - new_top)
        factor = jnp.exp(old_top - new_top)
        top[...] = new_top
        total[...] = total[...] * factor + jnp.sum(weights, axis=0, keepdims=True)
        acc[...] = acc[...] * factor + contract(values, weights.astype(jnp.bfloat16), 0, 0)
        return carry

    lax.fori_loop(bounds_ref[0], bounds_ref[1], step, 0)
    lse_ref[0] = top[...] + jnp.log(total[...])
    o_ref[...] = unstack_pair(acc[...] / total[...], rows).T


def backward_kernel(
    tile_rows, bounds_ref, q_ref, k_ref, v_ref, g_ref, o_ref, lse_ref, starts_ref, places_ref,
    dq_ref, dk_ref, dv_ref, acc,
):
    rows = q_ref.shape[0]
    stacked = stack_pair(q_ref[...])
    grads = g_ref[...]
    stacked_g = stack_pair(grads)
    mixed = (grads.astype(jnp.float32) * o_ref[...]).T
    half = mixed.shape[0] // 2
    row_dots = jnp.concatenate(
        [
            jnp.sum(mixed[:half], axis=0, keepdims=True),
            jnp.sum(mixed[half:], axis=0, keepdims=True),
        ],
        axis=1,
    )
    starts = starts_ref[...]
    places = places_ref[...]
    totals = lse_ref[0]
    acc[...] = jnp.zeros_like(acc)
    dk_ref[...] = jnp.zeros_like(dk_ref)
    dv_ref[...] = jnp.zeros_like(dv_ref)

    def step(tile, carry):
        offset = pl.multiple_of(tile * tile_rows, tile_rows)
        keys = k_ref[pl.ds(offset, tile_rows), :]
        values = v_ref[pl.ds(offset, tile_rows), :]
        scores = masked_scores(bounds_ref, keys, stacked, starts, places, offset)
        probs = jnp.exp(scores - totals)
        d_probs = contract(values, stacked_g, 1, 1)
        d_scores = (probs * (d_probs - row_dots)).astype(jnp.bfloat16)
        dv_ref[pl.ds(offset, tile_rows), :] = contract(
            probs.astype(jnp.bfloat16), stacked_g, 1, 0
        ).astype(dv_ref.dtype)
        dk_ref[pl.ds(offset, tile_rows), :] = contract(d_scores, stacked, 1, 0).astype(dk_ref.dtype)
        acc[...] += contract(keys, d_scores, 0, 0)
        return carry

    lax.fori_loop(bounds_ref[0], bounds_ref[1], step, 0)
    dq_ref[...] = unstack_pair(acc[...], rows).T


def column_spec(rows, first=0):
    return pl.BlockSpec((rows, LANES), lambda pair, bounds: (0, first + pair))


def whole_spec(cols):
    return pl.BlockSpec((1, cols), lambda pair, bounds: (0, 0))


def pair_spec(cols):
    return pl.BlockSpec((1, 1, cols), lambda pair, bounds: (pair, 0, 0))


def attend(tile_rows, bounds, queries, keys_values, starts, places):
    rows, width = queries.shape
    length = keys_values.shape[0]
    pairs = width // LANES
    return pl.pallas_call(
        functools.partial(forward_kernel, tile_rows),
        grid_spec=pltpu.PrefetchScalarGridSpec(
            num_scalar_prefetch=1,
            grid=(pairs,),
            in_specs=[
                column_spec(rows), column_spec(length), column_spec(length, pairs),
                whole_spec(2 * rows), whole_spec(2 * rows),
            ],
            out_specs=[column_spec(rows), pair_spec(2 * rows)],
            scratch_shapes=[
                pltpu.VMEM((1, 2 * rows), jnp.float32),
                pltpu.VMEM((1, 2 * rows), jnp.float32),
                pltpu.VMEM((LANES, 2 * rows), jnp.float32),
            ],
        ),
        out_shape=[
            jax.ShapeDtypeStruct((rows, width), jnp.float32),
            jax.ShapeDtypeStruct((pairs, 1, 2 * rows), jnp.float32),
        ],
        compiler_params=pltpu.CompilerParams(vmem_limit_bytes=40 * 1024 * 1024),
        cost_estimate=pl.CostEstimate(
            flops=8 * rows * length * width, bytes_accessed=8 * length * width,
            transcendentals=rows * length * width // 64,
        ),
        name="attention_forward",
    )(bounds, queries, keys_values, keys_values, starts, places)


def attend_back(tile_rows, bounds, queries, keys_values, grads, mixed, totals, starts, places):
    rows, width = queries.shape
    length = keys_values.shape[0]
    pairs = width // LANES
    return pl.pallas_call(
        functools.partial(backward_kernel, tile_rows),
        grid_spec=pltpu.PrefetchScalarGridSpec(
            num_scalar_prefetch=1,
            grid=(pairs,),
            in_specs=[
                column_spec(rows), column_spec(length), column_spec(length, pairs),
                column_spec(rows), column_spec(rows), pair_spec(2 * rows),
                whole_spec(2 * rows), whole_spec(2 * rows),
            ],
            out_specs=[column_spec(rows), column_spec(length), column_spec(length)],
            scratch_shapes=[pltpu.VMEM((LANES, 2 * rows), jnp.float32)],
        ),
        out_shape=[
            jax.ShapeDtypeStruct((rows, width), jnp.float32),
            jax.ShapeDtypeStruct((length, width), jnp.bfloat16),
            jax.ShapeDtypeStruct((length, width), jnp.bfloat16),
        ],
        compiler_params=pltpu.CompilerParams(vmem_limit_bytes=48 * 1024 * 1024),
        cost_estimate=pl.CostEstimate(
            flops=20 * rows * length * width, bytes_accessed=12 * length * width,
            transcendentals=rows * length * width // 64,
        ),
        name="attention_backward",
    )(bounds, queries, keys_values, keys_values, grads, mixed, totals, starts, places)


def body(hidden_in, segments, cotangent, w_qkv, w_out, w_up, w_down, vectors):
    tok_rows = hidden_in.shape[1]
    model_width = hidden_in.shape[2]
    head_dim = model_width // HEADS
    score_scale = head_dim ** (-0.5)
    length = segments.shape[1]
    spread_count = lax.axis_size("dp") * lax.axis_size("seq")
    seg_row = segments[0]
    query_first = lax.axis_index("seq") * tok_rows
    query_places = query_first + jnp.arange(tok_rows, dtype=jnp.int32)
    query_segs = lax.dynamic_slice_in_dim(seg_row, query_first, tok_rows)
    fwd_gathered = fetch(w_qkv, w_out, w_up, w_down, vectors)
    fwd_weights = shape_weights(fwd_gathered, model_width)
    hidden_units = FF
    (
        gain_one,
        shift_one,
        bias_query,
        bias_value,
        bias_proj,
        gain_two,
        shift_two,
        bias_up,
        bias_down,
    ) = unpack(fwd_weights[4].reshape(-1).astype(jnp.float32), model_width, hidden_units)
    tokens = hidden_in[0].astype(jnp.float32)
    normed_f, pull_one = jax.vjp(layer_norm, tokens, gain_one, shift_one)
    normed = normed_f.astype(jnp.bfloat16)
    packed = jnp.dot(normed, fwd_weights[0], preferred_element_type=jnp.float32)
    queries = (packed[:, :model_width] + bias_query).astype(jnp.bfloat16)
    key_rows = packed[:, model_width : 2 * model_width].astype(jnp.bfloat16)
    value_rows = (packed[:, 2 * model_width :] + bias_value).astype(jnp.bfloat16)
    pair_width = pl.cdiv(model_width, LANES) * LANES

    def widen(matrix):
        return jnp.pad(matrix, ((0, 0), (0, pair_width - matrix.shape[1])))

    queries = widen(queries * jnp.bfloat16(score_scale))
    key_rows = widen(key_rows)
    value_rows = widen(value_rows)
    ranks = lax.axis_size("seq")
    behind = min(ranks - 1, pl.cdiv(SEGMENT_MOST - 1, tok_rows))
    tile_rows = math.gcd(tok_rows, 256)
    window_first = query_first - behind * tok_rows
    query_starts = jnp.sum(
        (seg_row[None, :] < query_segs[:, None]).astype(jnp.int32), axis=1, dtype=jnp.int32
    )
    query_starts = query_starts - window_first
    bounds = jnp.stack(
        [query_starts[0] // tile_rows, jnp.int32((behind + 1) * tok_rows // tile_rows)]
    )
    starts = jnp.tile(query_starts, 2)[None]
    places = jnp.tile(query_places - window_first, 2)[None]
    own_pair = jnp.concatenate([key_rows, value_rows], axis=1)
    window = [own_pair]
    for back in range(1, behind + 1):
        pairs = [(rank, rank + back) for rank in range(ranks - back)]
        window.insert(0, lax.ppermute(own_pair, "seq", pairs))
    keys_values = jnp.concatenate(window, axis=0)
    attended_f, log_total = attend(tile_rows, bounds, queries, keys_values, starts, places)
    attended = attended_f[:, :model_width].astype(jnp.bfloat16)
    middle = (
        tokens + jnp.dot(attended, fwd_weights[1], preferred_element_type=jnp.float32) + bias_proj
    )
    normed_two_f, pull_two = jax.vjp(layer_norm, middle, gain_two, shift_two)
    normed_two = normed_two_f.astype(jnp.bfloat16)
    before = jnp.dot(normed_two, fwd_weights[2], preferred_element_type=jnp.float32) + bias_up
    active_f, pull_gelu = jax.vjp(jax.nn.gelu, before)
    active = active_f.astype(jnp.bfloat16)
    result = (
        middle + jnp.dot(active, fwd_weights[3], preferred_element_type=jnp.float32) + bias_down
    )
    hidden_out = result.astype(jnp.bfloat16)[None]
    back_weights = fwd_weights
    cot_rows = cotangent[0]
    cot_float = cot_rows.astype(jnp.float32)
    grad_down_full = jnp.dot(active.T, cot_rows, preferred_element_type=jnp.float32)
    d_bias_down = jnp.sum(cot_float, axis=0)
    d_active = jnp.dot(cot_rows, back_weights[3].T, preferred_element_type=jnp.float32)
    d_before = pull_gelu(d_active)[0].astype(jnp.bfloat16)
    d_bias_up = jnp.sum(d_before.astype(jnp.float32), axis=0)
    grad_up_full = jnp.dot(normed_two.T, d_before, preferred_element_type=jnp.float32)
    d_normed_two = jnp.dot(d_before, back_weights[2].T, preferred_element_type=jnp.float32)
    d_middle_norm, d_gain_two, d_shift_two = pull_two(d_normed_two)
    d_middle = cot_float + d_middle_norm
    grad_down = scatter_sum(to_flat(grad_down_full, w_down.shape[0] * spread_count))
    grad_up = scatter_sum(to_flat(grad_up_full, w_up.shape[0] * spread_count))
    d_proj = d_middle.astype(jnp.bfloat16)
    d_bias_proj = jnp.sum(d_middle, axis=0)
    grad_out_full = jnp.dot(attended.T, d_proj, preferred_element_type=jnp.float32)
    d_attended = jnp.dot(d_proj, back_weights[1].T, preferred_element_type=jnp.float32).astype(
        jnp.bfloat16
    )
    dq_sum, key_terms, value_terms = attend_back(
        tile_rows, bounds, queries, keys_values, widen(d_attended), attended_f, log_total, starts,
        places,
    )

    def to_owner(terms):
        total = terms[behind * tok_rows :].astype(jnp.float32)
        for back in range(1, behind + 1):
            piece = terms[(behind - back) * tok_rows : (behind - back + 1) * tok_rows]
            pairs = [(rank, rank - back) for rank in range(back, ranks)]
            total = total + lax.ppermute(piece, "seq", pairs).astype(jnp.float32)
        return total[:, :model_width].astype(jnp.bfloat16)

    d_key = to_owner(key_terms)
    d_value = to_owner(value_terms)
    d_query = (score_scale * dq_sum[:, :model_width]).astype(jnp.bfloat16)
    d_packed = jnp.concatenate([d_query, d_key, d_value], axis=1)
    grad_qkv_full = jnp.dot(normed.T, d_packed, preferred_element_type=jnp.float32)
    d_normed = jnp.dot(d_packed, back_weights[0].T, preferred_element_type=jnp.float32)
    d_tokens_norm, d_gain_one, d_shift_one = pull_one(d_normed)
    grad_in = (d_middle + d_tokens_norm)[None]
    vector_grads = jnp.concatenate(
        [
            d_gain_one,
            d_shift_one,
            jnp.sum(d_query.astype(jnp.float32), axis=0),
            jnp.sum(d_value.astype(jnp.float32), axis=0),
            d_bias_proj,
            d_gain_two,
            d_shift_two,
            d_bias_up,
            d_bias_down,
        ]
    )
    grad_out = scatter_sum(to_flat(grad_out_full, w_out.shape[0] * spread_count))
    grad_qkv = scatter_sum(to_flat(grad_qkv_full, w_qkv.shape[0] * spread_count))
    grad_vec = scatter_sum(
        to_flat(vector_grads, vectors.shape[0] * spread_count), jnp.float32
    )
    return (hidden_out, grad_in, grad_qkv, grad_out, grad_up, grad_down, grad_vec)


def solution(mesh):
    return jax.shard_map(
        body,
        mesh=mesh,
        in_specs=(
            P("dp", "seq", None),
            P("dp", None),
            P("dp", "seq", None),
            P(("dp", "seq"), None),
            P(("dp", "seq"), None),
            P(("dp", "seq"), None),
            P(("dp", "seq"), None),
            P(("dp", "seq"), None),
        ),
        out_specs=(
            P("dp", "seq", None),
            P("dp", "seq", None),
            P(("dp", "seq"), None),
            P(("dp", "seq"), None),
            P(("dp", "seq"), None),
            P(("dp", "seq"), None),
            P(("dp", "seq"), None),
        ),
        check_vma=False,
    )
```
